32 devices in a mesh: fsdp: 4 (over y, x), seq: 8 (over z, core).
Axes of the slice: x: 2, y: 2, z: 4, core: 2. Of those that a mesh axis runs over, the one named last changes fastest.
Arguments:
- inputs: bfloat16 [16, 1024, 1024], P('fsdp', 'seq'), may hold values from -6 to 6
- block_ids: int32 [16, 1024], P('fsdp'), may hold values from 0 to 5, never falling along the last dimension, each value on 1 to 256 neighbouring positions
- cotangent: bfloat16 [16, 1024, 1024], P('fsdp', 'seq'), may hold values from -6 to 6
- w_query: bfloat16 [1024, 1024], P(('fsdp', 'seq')), may hold values from -0.1875 to 0.1875
- w_key: bfloat16 [1024, 1024], P(('fsdp', 'seq')), may hold values from -0.1875 to 0.1875
- w_value: bfloat16 [1024, 1024], P(('fsdp', 'seq')), may hold values from -0.1875 to 0.1875
- w_out: bfloat16 [1024, 1024], P(('fsdp', 'seq')), may hold values from -0.75 to 0.75
- w_gate: bfloat16 [1024, 4096], P(('fsdp', 'seq')), may hold values from -0.1875 to 0.1875
- w_up: bfloat16 [1024, 4096], P(('fsdp', 'seq')), may hold values from -0.1875 to 0.1875
- w_down: bfloat16 [4096, 1024], P(('fsdp', 'seq')), may hold values from -0.09375 to 0.09375
- gain_attn: bfloat16 [1024], P(('fsdp', 'seq')), may hold values from 0.5 to 1.5
- gain_ffn: bfloat16 [1024], P(('fsdp', 'seq')), may hold values from 0.5 to 1.5
Outputs:
- layer_out: bfloat16 [16, 1024, 1024], P('fsdp', 'seq')
- grad_inputs: float32 [16, 1024, 1024], P('fsdp', 'seq')
- grad_w_query: float32 [1024, 1024], P(('fsdp', 'seq'))
- grad_w_key: float32 [1024, 1024], P(('fsdp', 'seq'))
- grad_w_value: float32 [1024, 1024], P(('fsdp', 'seq'))
- grad_w_out: float32 [1024, 1024], P(('fsdp', 'seq'))
- grad_w_gate: float32 [1024, 4096], P(('fsdp', 'seq'))
- grad_w_up: float32 [1024, 4096], P(('fsdp', 'seq'))
- grad_w_down: float32 [4096, 1024], P(('fsdp', 'seq'))
- grad_gain_attn: float32 [1024], P(('fsdp', 'seq'))
- grad_gain_ffn: float32 [1024], P(('fsdp', 'seq'))
The draws below stay inside these ranges and needn't reach their ends.
Inputs may be any that keep to these rules, and one draw needn't show every extreme that they name: `block_ids`: along each sequence the block numbers start at 0, never fall and rise by one from block to block; a block holds 1 to 256 tokens, and some block of each sequence holds exactly 256.
All inputs are finite; a program needn't handle non-finite values.
Results may differ from the reference program's by a relative error of at most 0.014.
Values may be sent and summed in bfloat16 or wider, within the bound.
No kernel may reach another device: no remote copies, remote signals or barrier semaphores. Data moves between devices by JAX's collectives and lax.ppermute only.
A program may use at most 192 MiB of HBM per device.

```python
import math
import jax
import jax.numpy as jnp
import numpy as np
from jax import lax

D = 1024
H = 16
HD = 64
FF = 4096
BLK = 256
SEQ_LEN = 1024
SEQUENCES = 16


def strengthened(values, own_key, source, target, parts, factor):
    owner, partner = [(jnp.arange(values.shape[axis_at]) // (values.shape[axis_at] // parts)).reshape([-1 if axis == axis_at else 1 for axis in range(values.ndim)]) for axis_at in (source, target)]
    chosen = jax.random.permutation(own_key, parts)[partner]
    strong = (owner == chosen) | (owner == (partner + parts // 2) % parts)
    return jnp.where(strong, factor * values, values)


def steps_of(key, shape, cuts, low, largest):
    level, own = 1.0, jax.random.fold_in(key, 6)
    for position, shards_of in cuts:
        draws = jnp.exp(jax.random.uniform(jax.random.fold_in(own, position), (shards_of,), jnp.float32, low / len(cuts), largest / len(cuts)))
        level = level * jnp.repeat(draws, shape[position] // shards_of).reshape([-1 if axis == position else 1 for axis in range(len(shape))])
    return level


def profile(count, total, limit, slope):
    portions = [(1 << 20) // math.isqrt(grade ** slope) + 1 for grade in range(2, count + 1)]
    rest, counts = total - limit - (count - 1), [1] * (count - 1)
    while rest > 0:
        movable = [i for i in range(count - 1) if counts[i] < limit]
        whole, budget = sum([portions[i] for i in movable]), rest
        for i in movable:
            more = min(limit - counts[i], max(1, budget * portions[i] // whole), rest)
            counts[i] = counts[i] + more
            rest = rest - more
    return np.array([limit] + counts)


def ragged(rng, amount, total, bound, skew):
    if amount == 2:
        one = jax.random.randint(rng, (), max(1, total - bound), min(bound, total - 1) + 1)
        return jnp.stack([one, total - one])
    tallies = jnp.asarray(profile(amount, total, bound, skew), jnp.int32)
    couples = (amount - 1) // 2
    donor, taker = tallies[1:1 + 2 * couples:2], tallies[2:2 + 2 * couples:2]
    margin = jnp.minimum(donor - 1, bound - taker)
    moved = jax.random.randint(jax.random.fold_in(rng, 1), (couples,), 0, 1 << 20) % (margin + 1)
    tallies = tallies.at[1:1 + 2 * couples:2].set(donor - moved).at[2:2 + 2 * couples:2].set(taker + moved)
    return tallies[jax.random.permutation(jax.random.fold_in(rng, 2), amount)]


def centred(stream_key, dims, deviation, reach, shards=(), held_as=jnp.bfloat16):
    entries = deviation * jax.random.normal(stream_key, dims, jnp.float32)
    if shards:
        entries = entries * steps_of(stream_key, dims, shards, -0.22, 0.18)
    return jnp.clip(entries, -reach, reach).astype(held_as)


def noise_with(stream_key, dims, deviation, limit, cuts, heavy, held_as=jnp.bfloat16):
    array = deviation * jax.random.normal(stream_key, dims, jnp.float32)
    if cuts:
        array = array * steps_of(stream_key, dims, cuts, -0.22, 0.18)
    return jnp.clip(strengthened(array, jax.random.fold_in(stream_key, 3), *heavy), -limit, limit).astype(held_as)


def setup_inputs(seed: int = 0) -> dict:
    seeds = jax.random.split(jax.random.key(seed), 13)
    return {
        "inputs": noise_with(seeds[0], (SEQUENCES, SEQ_LEN, D), 1.0, 6.0, ((0, 4), (1, 8)), (1, 2, 8, 2.0)),
        "block_ids": jax.vmap(lambda own: jnp.searchsorted(jnp.cumsum(ragged(own, SEQ_LEN // BLK + SEQ_LEN // (2 * BLK), SEQ_LEN, BLK, 1)), jnp.arange(SEQ_LEN), side="right"))(jax.random.split(seeds[1], SEQUENCES)).reshape((SEQUENCES, SEQ_LEN)).astype(jnp.int32),
        "cotangent": centred(seeds[2], (SEQUENCES, SEQ_LEN, D), 1.0, 6.0, ((0, 4), (1, 8))),
        "w_query": centred(seeds[3], (D, D), D ** -0.5, 0.1875, ((0, 32),)),
        "w_key": centred(seeds[4], (D, D), D ** -0.5, 0.1875, ((0, 32),)),
        "w_value": centred(seeds[5], (D, D), D ** -0.5, 0.1875, ((0, 32),)),
        "w_out": centred(seeds[6], (D, D), (D // 16) ** -0.5, 0.75, ((0, 32),)),
        "w_gate": centred(seeds[7], (D, FF), D ** -0.5, 0.1875, ((0, 32),)),
        "w_up": centred(seeds[8], (D, FF), D ** -0.5, 0.1875, ((0, 32),)),
        "w_down": centred(seeds[9], (FF, D), FF ** -0.5, 0.09375, ((0, 32),)),
        "gain_attn": jnp.clip(1.0 + 0.1 * jax.random.normal(seeds[10], (D,), jnp.float32), 0.5, 1.5).astype(jnp.bfloat16),
        "gain_ffn": jnp.clip(1.0 + 0.1 * jax.random.normal(seeds[11], (D,), jnp.float32), 0.5, 1.5).astype(jnp.bfloat16),
    }


highest = lax.Precision.HIGHEST
norm_eps = 1e-05
masked_fill = -1e+30

@jax.custom_vjp
def low(v):
    return lax.optimization_barrier(v.astype(jnp.bfloat16)).astype(jnp.float32)

@jax.custom_vjp
def low_back(v):
    return v

def low_keep(v):
    return (low(v), None)

def low_pass(kept, grad):
    return (grad,)

def back_keep(v):
    return (v, None)

def back_low(kept, grad):
    return (low(grad),)
low.defvjp(low_keep, low_pass)
low_back.defvjp(back_keep, back_low)

def rms_scale(values, gain):
    return values * lax.rsqrt(lax.optimization_barrier(jnp.mean(values * values, axis=-1, keepdims=True)) + norm_eps) * gain

def silu_mul(gate_raw, up_raw):
    return jax.nn.silu(gate_raw) * up_raw

def forward_layer(inputs, block_ids, w_query, w_key, w_value, w_out, w_gate, w_up, w_down, gain_attn, gain_ffn):
    group_size, seq_len, feature_width = inputs.shape
    normed = low(rms_scale(inputs, gain_attn))

    def project(matrix):
        raw_proj = jnp.einsum('gtd,de->gte', normed, matrix, precision=highest)
        return low(low_back(raw_proj)).reshape(group_size, seq_len, H, HD)
    query = project(w_query)
    keyed = project(w_key)
    valued = project(w_value)
    row_count = min(512, seq_len)
    block_count = seq_len // row_count
    score_scale = HD ** (-0.5)

    def attend(block_index):
        offset = block_index * row_count
        query_rows = lax.dynamic_slice_in_dim(query, offset, row_count, 1)
        block_rows = lax.dynamic_slice_in_dim(block_ids, offset, row_count, 1)
        scores = low_back(jnp.einsum('gqhc,gkhc->ghqk', query_rows, keyed, precision=highest) * score_scale)
        allowed = block_ids[:, None, None, :] <= block_rows[:, None, :, None]
        scores = jnp.where(allowed, scores, masked_fill)
        attn_probs = low(jax.nn.softmax(scores, axis=-1))
        return jnp.einsum('ghqk,gkhc->gqhc', attn_probs, valued, precision=highest)
    pieces = lax.map(jax.checkpoint(attend), jnp.arange(block_count, dtype=jnp.int32))
    attended = jnp.moveaxis(pieces, 0, 1).reshape(group_size, seq_len, feature_width)
    attended = low(low_back(attended))
    middle = inputs + low_back(jnp.einsum('gte,ed->gtd', attended, w_out, precision=highest))
    normed_ffn = low(rms_scale(middle, gain_ffn))
    gate_raw = low_back(jnp.einsum('gtd,df->gtf', normed_ffn, w_gate, precision=highest))
    up_raw = low_back(jnp.einsum('gtd,df->gtf', normed_ffn, w_up, precision=highest))
    hidden = low(silu_mul(gate_raw, up_raw))
    return middle + low_back(jnp.einsum('gtf,fd->gtd', hidden, w_down, precision=highest))

def reference(inputs, block_ids, cotangent, w_query, w_key, w_value, w_out, w_gate, w_up, w_down, gain_attn, gain_ffn):
    group_size = math.gcd(SEQUENCES, max(1, 4096 // SEQ_LEN))
    group_count = SEQUENCES // group_size
    weights = tuple((matrix.astype(jnp.float32) for matrix in (w_query, w_key, w_value, w_out, w_gate, w_up, w_down, gain_attn, gain_ffn)))
    shaped_in = inputs.astype(jnp.float32).reshape(group_count, group_size, SEQ_LEN, D)
    shaped_ids = block_ids.astype(jnp.int32).reshape(group_count, group_size, SEQ_LEN)
    shaped_cot = cotangent.astype(jnp.float32).reshape(group_count, group_size, SEQ_LEN, D)

    def one_group(summed, group_item):
        group_in, group_ids, group_cot = group_item

        def apply_layer(values, p_query, p_key, p_value, p_out, p_gate, p_up, p_down, p_gain_attn, p_gain_ffn):
            return forward_layer(values, group_ids, p_query, p_key, p_value, p_out, p_gate, p_up, p_down, p_gain_attn, p_gain_ffn)
        result, pull_back = jax.vjp(apply_layer, group_in, *weights)
        grads = pull_back(group_cot)
        summed = tuple((total_grad + group_grad for total_grad, group_grad in zip(summed, grads[1:])))
        return (summed, (result.astype(jnp.bfloat16), grads[0]))
    zeros = tuple((jnp.zeros(matrix.shape, jnp.float32) for matrix in weights))
    summed, (layer_out, grad_inputs) = lax.scan(one_group, zeros, (shaped_in, shaped_ids, shaped_cot))
    return (layer_out.reshape(SEQUENCES, SEQ_LEN, D), grad_inputs.reshape(SEQUENCES, SEQ_LEN, D), summed[0], summed[1], summed[2], summed[3], summed[4], summed[5], summed[6], summed[7], summed[8])
```

```python
import functools

import jax
import jax.numpy as jnp
from jax import lax
from jax.experimental import pallas as pl
from jax.experimental.pallas import tpu as pltpu
from jax.sharding import Mesh
from jax.sharding import PartitionSpec as P


HD = 64
BLK = 256
PAIR = 128
norm_eps = 1e-05
masked_fill = -1e30
bf16 = jnp.bfloat16
f32 = jnp.float32


def dot(a, b, dims):
    return lax.dot_general(a, b, (dims, ((), ())), preferred_element_type=f32)


def nn(a, b):
    return dot(a, b, ((1,), (0,)))


def nt(a, b):
    return dot(a, b, ((1,), (1,)))


def tn(a, b):
    return dot(a, b, ((0,), (0,)))


def head_masks():
    lane = lax.broadcasted_iota(jnp.int32, (1, PAIR), 1)
    return [(lane // HD) == h for h in range(PAIR // HD)]


def attend_kernel(qkv_ref, ids_row_ref, ids_col_ref, out_ref, lse_ref):
    seq_len = qkv_ref.shape[0]
    scale = HD ** (-0.5)
    masks = head_masks()
    value_t = qkv_ref[:, 2 * PAIR : 3 * PAIR].T
    for i in range(seq_len // BLK):
        low, high = i * BLK, min(seq_len, (i + 2) * BLK)
        query = qkv_ref[low : low + BLK, 0:PAIR] * jnp.asarray(scale, bf16)
        allowed = ids_col_ref[low:high, :] <= ids_row_ref[:, low : low + BLK]
        parts = []
        for h, mask in enumerate(masks):
            own = jnp.where(mask, query, jnp.zeros_like(query))
            near = nt(qkv_ref[low:high, PAIR : 2 * PAIR], own)
            near = jnp.where(allowed, near, masked_fill)
            top = jnp.max(near, axis=0, keepdims=True)
            if low:
                far = nt(qkv_ref[0:low, PAIR : 2 * PAIR], own)
                top = jnp.maximum(top, jnp.max(far, axis=0, keepdims=True))
            near = jnp.exp(near - top)
            total = jnp.sum(near, axis=0, keepdims=True)
            mixed = nn(value_t[:, low:high], near.astype(bf16))
            if low:
                far = jnp.exp(far - top)
                total = total + jnp.sum(far, axis=0, keepdims=True)
                mixed = mixed + nn(value_t[:, 0:low], far.astype(bf16))
            mixed = mixed / total
            parts.append(mixed[h * HD : (h + 1) * HD, :])
            lse_ref[0, h : h + 1, low : low + BLK] = top + jnp.log(total)
        out_ref[low : low + BLK, :] = jnp.concatenate(parts, axis=0).T.astype(bf16)


def attend_forward(qkv, ids):
    seq_len = qkv.shape[0]
    pairs = qkv.shape[1] // (3 * PAIR)
    return pl.pallas_call(
        attend_kernel,
        grid=(pairs,),
        in_specs=[
            pl.BlockSpec((seq_len, 3 * PAIR), lambda p: (0, p)),
            pl.BlockSpec((1, seq_len), lambda p: (0, 0)),
            pl.BlockSpec((seq_len, 1), lambda p: (0, 0)),
        ],
        out_specs=[
            pl.BlockSpec((seq_len, PAIR), lambda p: (0, p)),
            pl.BlockSpec((1, 8, seq_len), lambda p: (p, 0, 0)),
        ],
        out_shape=[
            jax.ShapeDtypeStruct((seq_len, pairs * PAIR), bf16),
            jax.ShapeDtypeStruct((pairs, 8, seq_len), f32),
        ],
        name="attend_fwd",
    )(qkv, ids.reshape(1, seq_len), ids.reshape(seq_len, 1))


def attend_back_kernel(
    qkv_ref, grad_ref, out_ref, lse_ref, ids_row_ref, ids_col_ref, dqkv_ref, dk_ref, dv_ref
):
    seq_len = qkv_ref.shape[0]
    scale = HD ** (-0.5)
    masks = head_masks()
    key_t = qkv_ref[:, PAIR : 2 * PAIR].T
    dk_ref[...] = jnp.zeros_like(dk_ref)
    dv_ref[...] = jnp.zeros_like(dv_ref)
    for i in range(seq_len // BLK):
        low, high = i * BLK, min(seq_len, (i + 2) * BLK)
        rows = slice(low, low + BLK)
        query = qkv_ref[rows, 0:PAIR] * jnp.asarray(scale, bf16)
        grad = grad_ref[rows, :]
        allowed = ids_col_ref[low:high, :] <= ids_row_ref[:, rows]
        weighted = (grad.astype(f32) * out_ref[rows, :].astype(f32)).T
        parts = []
        for h, mask in enumerate(masks):
            own_q = jnp.where(mask, query, jnp.zeros_like(query))
            own_g = jnp.where(mask, grad, jnp.zeros_like(grad))
            lse = lse_ref[0, h : h + 1, rows]
            delta = jnp.sum(weighted[h * HD : (h + 1) * HD, :], axis=0, keepdims=True)
            dq = None
            for start, stop in ((low, high), (0, low)):
                if start == stop:
                    continue
                keys = slice(start, stop)
                scores = nt(qkv_ref[keys, PAIR : 2 * PAIR], own_q)
                if start == low:
                    scores = jnp.where(allowed, scores, masked_fill)
                probs = jnp.exp(scores - lse)
                d_probs = nt(qkv_ref[keys, 2 * PAIR : 3 * PAIR], own_g)
                d_scores = (probs * (d_probs - delta)).astype(bf16)
                dv_ref[keys, :] += nn(probs.astype(bf16), own_g)
                dk_ref[keys, :] += nn(d_scores, own_q)
                part = nn(key_t[:, keys], d_scores)
                dq = part if dq is None else dq + part
            parts.append(dq[h * HD : (h + 1) * HD, :])
        dqkv_ref[rows, 0:PAIR] = (jnp.concatenate(parts, axis=0) * scale).T.astype(bf16)
    dqkv_ref[:, PAIR : 2 * PAIR] = dk_ref[...].astype(bf16)
    dqkv_ref[:, 2 * PAIR : 3 * PAIR] = dv_ref[...].astype(bf16)


def attend_backward(qkv, grad, out, lse, ids):
    seq_len = qkv.shape[0]
    pairs = qkv.shape[1] // (3 * PAIR)
    wide = pl.BlockSpec((seq_len, 3 * PAIR), lambda p: (0, p))
    narrow = pl.BlockSpec((seq_len, PAIR), lambda p: (0, p))
    return pl.pallas_call(
        attend_back_kernel,
        grid=(pairs,),
        in_specs=[
            wide,
            narrow,
            narrow,
            pl.BlockSpec((1, 8, seq_len), lambda p: (p, 0, 0)),
            pl.BlockSpec((1, seq_len), lambda p: (0, 0)),
            pl.BlockSpec((seq_len, 1), lambda p: (0, 0)),
        ],
        out_specs=wide,
        out_shape=jax.ShapeDtypeStruct(qkv.shape, bf16),
        scratch_shapes=[pltpu.VMEM((seq_len, PAIR), f32), pltpu.VMEM((seq_len, PAIR), f32)],
        name="attend_bwd",
    )(qkv, grad, out, lse, ids.reshape(1, seq_len), ids.reshape(seq_len, 1))


def ffn_kernel(first, rows, tiles, *refs):
    if first:
        nf_ref, dy_ref, a_ref, b_ref, y_ref, d_ref, ga_ref, gb_ref, sa, sb = refs
    else:
        nf_ref, dy_ref, a_ref, b_ref, y_in, d_in, y_ref, d_ref, ga_ref, gb_ref, sa, sb = refs
    chips, stack, width = a_ref.shape
    feats = chips * rows
    down = tiles * rows
    span = chips // tiles

    @pl.when(pl.program_id(0) == 0)
    def _():
        sa[...] = jnp.zeros_like(sa)
        sb[...] = jnp.zeros_like(sb)

    nf = nf_ref[...]
    dy = dy_ref[...]
    dy_a, dy_b = dy[:, :width], dy[:, width:]
    y_a = y_b = d_nf = None

    def plus(total, part):
        return part if total is None else total + part

    for t in range(tiles):
        mine = slice(t * rows, (t + 1) * rows)
        those = slice(t * span, (t + 1) * span)
        w_gate = a_ref[:, mine, :].reshape(feats, width)
        w_up = b_ref[:, mine, :].reshape(feats, width)
        w_down_a = a_ref[those, down:, :].reshape(width, width)
        w_down_b = b_ref[those, down:, :].reshape(width, width)
        gate = nn(nf, w_gate)
        up = nn(nf, w_up)
        d_hidden = nt(dy_a, w_down_a) + nt(dy_b, w_down_b)
        sig = 1.0 / (1.0 + jnp.exp(-gate))
        silu = gate * sig
        hidden = (silu * up).astype(bf16)
        d_up = (d_hidden * silu).astype(bf16)
        d_gate = (d_hidden * up * (sig * (1.0 + gate * (1.0 - sig)))).astype(bf16)
        y_a = plus(y_a, nn(hidden, w_down_a))
        y_b = plus(y_b, nn(hidden, w_down_b))
        d_nf = plus(d_nf, nt(d_gate, w_gate) + nt(d_up, w_up))
        sa[:, mine, :] += tn(nf, d_gate).reshape(chips, rows, width)
        sb[:, mine, :] += tn(nf, d_up).reshape(chips, rows, width)
        sa[those, down:, :] += tn(hidden, dy_a).reshape(span, stack - down, width)
        sb[those, down:, :] += tn(hidden, dy_b).reshape(span, stack - down, width)
    if first:
        y_ref[:, :width] = y_a
        y_ref[:, width:] = y_b
        d_ref[...] = d_nf
    else:
        y_ref[:, :width] = y_in[:, :width] + y_a
        y_ref[:, width:] = y_in[:, width:] + y_b
        d_ref[...] = d_in[...] + d_nf

    @pl.when(pl.program_id(0) == pl.num_programs(0) - 1)
    def _():
        ga_ref[...] = sa[...].astype(bf16)
        gb_ref[...] = sb[...].astype(bf16)


def ffn_chunk(nf, dy, part_a, part_b, rows, tiles, sums):
    tokens, width = nf.shape
    tile = min(256, tokens)
    act = pl.BlockSpec((tile, width), lambda i: (i, 0))
    whole = pl.BlockSpec(part_a.shape, lambda i: (0, 0, 0))
    first = sums is None
    total = jax.ShapeDtypeStruct((tokens, width), f32)
    grads = jax.ShapeDtypeStruct(part_a.shape, bf16)
    return pl.pallas_call(
        functools.partial(ffn_kernel, first, rows, tiles),
        grid=(tokens // tile,),
        in_specs=[act, act, whole, whole] + ([] if first else [act, act]),
        out_specs=[act, act, whole, whole],
        out_shape=[total, total, grads, grads],
        scratch_shapes=[pltpu.VMEM(part_a.shape, f32), pltpu.VMEM(part_a.shape, f32)],
        input_output_aliases={} if first else {4: 0, 5: 1},
        compiler_params=pltpu.CompilerParams(vmem_limit_bytes=60 << 20),
        name="ffn",
    )(nf, dy, part_a, part_b, *(() if first else sums))


def shift(value, axis, step):
    size = lax.axis_size(axis)
    return lax.ppermute(value, axis, [(i, (i + step) % size) for i in range(size)])


def at(value, index, axis=0):
    return lax.dynamic_index_in_dim(value, index, axis, keepdims=False)


def ordered(pieces, axis, dim=0):
    size, own = len(pieces), lax.axis_index(axis)
    shape = list(pieces[0].shape)
    shape.insert(dim, size)
    out = jnp.zeros(shape, pieces[0].dtype)
    for step, piece in enumerate(pieces):
        where = (own - step) % size
        out = lax.dynamic_update_index_in_dim(out, piece, where, dim)
    return out


def share(value, axis):
    return [value] + [shift(value, axis, k) for k in range(1, lax.axis_size(axis))]


def swap(value, axis, dim=0):
    size, own = lax.axis_size(axis), lax.axis_index(axis)
    pieces = [at(value, own, dim)]
    for k in range(1, size):
        pieces.append(shift(at(value, (own + k) % size, dim), axis, k))
    return pieces


def gather_chips(value, order):
    names = ("fa", "fb", "sq")
    done = []
    for axis in order:
        dim = sum(names.index(have) < names.index(axis) for have in done)
        value = ordered(share(value, axis), axis, dim)
        done.append(axis)
    return value.reshape((-1,) + value.shape[3:])


def scatter_chips(value, order):
    names = ["fa", "fb", "sq"]
    left = [n for n in names]
    value = value.reshape(tuple(lax.axis_size(n) for n in names) + value.shape[1:])
    for axis in order:
        pieces = swap(value, axis, left.index(axis))
        total = pieces[0].astype(f32)
        for piece in pieces[1:]:
            total = total + piece.astype(f32)
        left.remove(axis)
        value = total.astype(value.dtype) if left else total
    return value


ORDER_A = ("sq", "fa", "fb")
ORDER_B = ("sq", "fb", "fa")


def after(value, *others):
    return lax.optimization_barrier((value,) + others)[0]


def inverse_rms(values):
    return lax.rsqrt(jnp.mean(values * values, axis=-1, keepdims=True) + norm_eps)


def rms_back(values, factor, gain, grad):
    unit = values * factor
    scaled = gain * grad
    d_values = factor * scaled - unit * jnp.mean(unit * scaled, axis=-1, keepdims=True) * factor
    return d_values, jnp.sum(unit * grad, axis=0)


def body(
    inputs,
    block_ids,
    cotangent,
    w_query,
    w_key,
    w_value,
    w_out,
    w_gate,
    w_up,
    w_down,
    gain_attn,
    gain_ffn,
):
    n_fa, n_fb, n_sq, n_tp = (lax.axis_size(name) for name in ("fa", "fb", "sq", "tp"))
    chips = n_fa * n_fb * n_sq
    sq, tp = lax.axis_index("sq"), lax.axis_index("tp")
    part_len, feats = inputs.shape[1:]
    seq_len = n_sq * n_tp * part_len
    half = feats // 2
    own_rows = w_query.shape[0]
    rows = own_rows * n_tp
    head_width = feats // n_tp
    pairs = head_width // PAIR
    pairs_a = pairs // 2
    cut = pairs_a * 3 * PAIR
    hidden_own = w_down.shape[0]
    chunks = max(1, hidden_own // 32)
    per_chip = hidden_own // chunks
    tiles = max(1, chips * per_chip // half)

    def spread(value):
        own = ordered(swap(value, "sq"), "sq")
        return own, ordered(share(own, "tp"), "tp", 1).reshape(seq_len, feats)

    columns = jnp.stack(
        [w.reshape(own_rows, n_tp, pairs, PAIR) for w in (w_query, w_key, w_value)], axis=3
    ).reshape(own_rows, n_tp, pairs * 3 * PAIR)
    gains = jnp.stack([gain_attn, gain_ffn], axis=1)
    gains = jnp.pad(gains, ((0, 0), (0, PAIR - 2)))
    gains = jnp.broadcast_to(gains[:, None, :], (own_rows, n_tp, PAIR))
    columns = jnp.concatenate([columns, gains], axis=2)
    columns = ordered(swap(columns, "tp", 1), "tp").reshape(rows, -1)
    qkv_a = gather_chips(columns[:, :cut], ORDER_A).reshape(feats, -1)
    qkv_b = gather_chips(columns[:, cut:], ORDER_B).reshape(feats, -1)

    x_own, x_low = spread(inputs)
    ids = at(block_ids, sq)
    x = x_low.astype(f32)

    gain_pair = qkv_b[:, -PAIR:].T[:2].astype(f32)
    g_attn, g_ffn = gain_pair[0:1], gain_pair[1:2]
    weights_qkv = (qkv_a, qkv_b[:, :-PAIR])
    normed = (x * inverse_rms(x) * g_attn).astype(bf16)
    qkv = [nn(normed, w).astype(bf16) for w in weights_qkv]
    attended, lse = zip(*[attend_forward(part, ids) for part in qkv])

    out_own = [
        gather_chips(w_out[:, :half], ORDER_A),
        gather_chips(w_out[:, half:], ORDER_B),
    ]
    out_own = jnp.concatenate(out_own, axis=2)
    out_full = ordered(share(out_own, "tp"), "tp", 1).reshape(feats, feats)

    block = half // per_chip

    def columns_of(w):
        w = w.reshape(own_rows, tiles, block, n_tp, chunks, per_chip)
        return w.transpose(3, 4, 1, 0, 2, 5).reshape(n_tp, chunks, tiles, own_rows, half)

    both = jnp.stack([columns_of(w_gate), columns_of(w_up)], axis=1)
    both = ordered(swap(both, "tp"), "tp", 3).reshape(2, chunks, tiles * rows, half)
    down = w_down.reshape(chunks, per_chip, feats)
    ffn_weights = []
    for q in range(chunks):
        stack_a = jnp.concatenate([both[0, q], down[q, :, :half]], axis=0)
        stack_b = jnp.concatenate([both[1, q], down[q, :, half:]], axis=0)
        ffn_weights.append((gather_chips(stack_a, ORDER_A), gather_chips(stack_b, ORDER_B)))

    _, dy_low = spread(cotangent)

    attended = jnp.concatenate(attended, axis=1)
    middle = x
    for k, piece in enumerate(share(attended, "tp")):
        place = ((tp - k) % n_tp) * head_width
        middle = middle + nn(piece, lax.dynamic_slice_in_dim(out_full, place, head_width, 0))
    factor_ffn = inverse_rms(middle)
    nf = (middle * factor_ffn * g_ffn).astype(bf16)

    sums, ffn_grads = None, []
    for part_a, part_b in ffn_weights:
        *sums, grad_a, grad_b = ffn_chunk(nf, dy_low, part_a, part_b, rows, tiles, sums)
        ffn_grads.append(
            (scatter_chips(grad_a, ORDER_A[::-1]), scatter_chips(grad_b, ORDER_B[::-1]))
        )
    y, d_nf = sums

    def halves(value, own):
        pieces = swap(value.reshape(n_sq, n_tp, part_len, feats), "tp", 1)
        for piece in pieces:
            own = own + piece.astype(f32)
        return own

    def own_tokens(value):
        return at(value.reshape(n_sq, n_tp, part_len, -1), tp, 1)

    d_nf_low = d_nf.astype(bf16)
    for k in range(1, n_tp):
        d_nf = d_nf + shift(d_nf_low, "tp", k).astype(f32)
    d_values, grad_g_ffn = rms_back(middle, factor_ffn, g_ffn, d_nf)
    d_middle = dy_low.astype(f32) + d_values
    d_branch = d_middle.astype(bf16)
    out_mine = lax.dynamic_slice_in_dim(out_full, tp * head_width, head_width, 0)
    d_attended = nt(d_branch, out_mine).astype(bf16)
    wide = pairs_a * PAIR
    d_qkv = [
        attend_backward(qkv[0], d_attended[:, :wide], attended[:, :wide], lse[0], ids),
        attend_backward(qkv[1], d_attended[:, wide:], attended[:, wide:], lse[1], ids),
    ]
    grad_out = tn(attended, d_branch).astype(bf16)
    grad_out = grad_out.reshape(chips // n_tp, n_tp, own_rows, feats)
    grad_out = ordered(swap(grad_out, "tp", 1), "tp").reshape(chips, own_rows, feats)
    grad_out = jnp.concatenate(
        [
            scatter_chips(grad_out[:, :, :half], ORDER_A[::-1]),
            scatter_chips(grad_out[:, :, half:], ORDER_B[::-1]),
        ],
        axis=1,
    )

    y_own = halves(y.astype(bf16), own_tokens(middle))
    layer_out = ordered(swap(y_own.astype(bf16), "sq"), "sq")

    grad_qkv = [
        scatter_chips(tn(normed, d).astype(bf16).reshape(chips, rows, -1), order[::-1])
        for d, order in zip(d_qkv, (ORDER_A, ORDER_B))
    ]
    d_normed = sum(nt(d, w) for d, w in zip(d_qkv, weights_qkv))
    d_normed = halves(d_normed.astype(bf16), jnp.zeros((), f32)).reshape(-1, feats)
    x_mine = x_own.reshape(-1, feats).astype(f32)
    d_values, grad_g_attn = rms_back(x_mine, inverse_rms(x_mine), g_attn, d_normed)
    d_inputs = own_tokens(d_middle) + d_values.reshape(n_sq, part_len, feats)
    grad_inputs = ordered(swap(d_inputs.astype(bf16), "sq"), "sq").astype(f32)

    pair = jnp.stack([grad_g_attn, grad_g_ffn * (1.0 / n_tp)], axis=0)
    pair = pair.reshape(2, chips, n_tp, own_rows).transpose(1, 2, 0, 3)
    pair = pair.reshape(chips, n_tp, 1, 2 * own_rows)
    pair = sum(swap(pair, "tp", 1))
    pair = scatter_chips(pair, ORDER_A[::-1]).reshape(2, own_rows)

    grad_cols = jnp.concatenate(grad_qkv, axis=1).reshape(n_tp, own_rows, pairs, 3, PAIR)
    grad_cols = ordered(swap(grad_cols, "tp"), "tp")
    grad_cols = grad_cols.transpose(3, 1, 0, 2, 4).reshape(3, own_rows, feats)

    kept = tiles * rows
    grad_both = jnp.stack(
        [jnp.stack([a[:kept], b[:kept]], axis=0) for a, b in ffn_grads], axis=0
    )
    grad_both = grad_both.reshape(chunks, 2, tiles, n_tp, own_rows, half)
    grad_both = ordered(swap(grad_both, "tp", 3), "tp")
    grad_both = grad_both.reshape(n_tp, chunks, 2, tiles, own_rows, block, per_chip)
    grad_both = grad_both.transpose(2, 4, 3, 5, 0, 1, 6).reshape(2, own_rows, -1)
    grad_down = jnp.concatenate(
        [jnp.concatenate([a[kept:], b[kept:]], axis=1) for a, b in ffn_grads], axis=0
    )

    return (
        layer_out,
        grad_inputs,
        grad_cols[0],
        grad_cols[1],
        grad_cols[2],
        grad_out,
        grad_both[0],
        grad_both[1],
        grad_down,
        pair[0],
        pair[1],
    )


def solution(mesh):
    n_fsdp, n_seq = mesh.shape["fsdp"], mesh.shape["seq"]

    def step(*args):
        group = args[0].shape[0] // n_fsdp
        shape = (2, n_fsdp // 2, group, n_seq // group)
        fine = Mesh(mesh.devices.reshape(shape), ("fa", "fb", "sq", "tp"))
        batch, tokens = ("fa", "fb"), ("sq", "tp")
        acts = P(batch, tokens, None)
        matrix, vector = P(batch + tokens, None), P(batch + tokens)
        return jax.shard_map(
            body,
            mesh=fine,
            in_specs=(acts, P(batch, None), acts) + (matrix,) * 7 + (vector,) * 2,
            out_specs=(acts, acts) + (matrix,) * 7 + (vector,) * 2,
            check_vma=False,
        )(*args)

    return step
```
